32 devices in a mesh: row: 4 (over y, x), col: 8 (over z, core).
Axes of the slice: x: 2, y: 2, z: 4, core: 2. Of those that a mesh axis runs over, the one named last changes fastest.
Arguments:
- tokens_in: bfloat16 [768, 8192], P('row', 'col'), may hold values from -6 to 6
- grad_out: bfloat16 [768, 8192], P('row', 'col'), may hold values from -1.5 to 1.5
- w_gate: bfloat16 [8192, 28672], P('col', 'row'), may hold values from -0.0625 to 0.0625
- w_up: bfloat16 [8192, 28672], P('col', 'row'), may hold values from -0.0625 to 0.0625
- w_down: bfloat16 [28672, 8192], P('row', 'col'), may hold values from -0.03125 to 0.03125
Outputs:
- grad_input: bfloat16 [768, 8192], P('row', 'col')
- grad_gate: bfloat16 [8192, 28672], P('col', 'row')
- grad_up: bfloat16 [8192, 28672], P('col', 'row')
- grad_down: bfloat16 [28672, 8192], P('row', 'col')
The draws below stay inside these ranges and needn't reach their ends.
All inputs are finite; a program needn't handle non-finite values.
Results may differ from the reference program's by a relative error of at most 0.023.
Values may be sent and summed in bfloat16 or wider, within the bound.
A program may use at most 256 MiB of HBM per device.

```python
import jax
import jax.numpy as jnp
from jax import lax

D = 8192
FF = 28672
TOKENS = 768
N_COL = 8


def block_scale(rng, extent, pieces, least, top_value):
    gain = 1.0
    for position, parts in pieces:
        steps = jax.random.uniform(jax.random.fold_in(jax.random.fold_in(rng, 6), position), (parts,), jnp.float32, least / len(pieces), top_value / len(pieces))
        gain = gain * jnp.repeat(jnp.exp(steps), extent[position] // parts).reshape((-1,) + (1,) * (len(extent) - 1 - position))
    return gain


def normal_values(rng, extent, width, most, shards=(), kind=jnp.bfloat16):
    array = width * jax.random.normal(rng, extent, jnp.float32)
    if shards:
        array = array * block_scale(rng, extent, shards, -0.22, 0.18)
    return jnp.clip(array, -most, most).astype(kind)


def setup_inputs(seed: int = 0) -> dict:
    seeds = jax.random.split(jax.random.key(seed), 6)
    tokens_in = normal_values(seeds[0], (TOKENS, D), 1.0, 6.0, ((0, 4), (1, 8)))
    grad_out = normal_values(seeds[1], (TOKENS, D), 0.25, 1.5, ((0, 4), (1, 8)))
    w_gate = normal_values(seeds[2], (D, FF), D ** -0.5, 0.0625, ((0, 8), (1, 4)))
    w_up = normal_values(seeds[3], (D, FF), D ** -0.5, 0.0625, ((0, 8), (1, 4)))
    w_down = normal_values(seeds[4], (FF, D), FF ** -0.5, 0.03125, ((0, 4), (1, 8)))
    return {"tokens_in": tokens_in, "grad_out": grad_out, "w_gate": w_gate, "w_up": w_up, "w_down": w_down}


def reference(tokens_in, grad_out, w_gate, w_up, w_down):
    block = D // N_COL

    def add_block(carry, index):
        start = (index * block).astype(jnp.int32)
        xs = lax.dynamic_slice_in_dim(tokens_in, start, block, 1)
        ds = lax.dynamic_slice_in_dim(grad_out, start, block, 1)
        wg = lax.dynamic_slice_in_dim(w_gate, start, block, 0)
        wu = lax.dynamic_slice_in_dim(w_up, start, block, 0)
        wd = lax.dynamic_slice_in_dim(w_down, start, block, 1)
        gate_k = jnp.dot(xs, wg, preferred_element_type=jnp.float32).astype(jnp.bfloat16)
        up_k = jnp.dot(xs, wu, preferred_element_type=jnp.float32).astype(jnp.bfloat16)
        back_k = jnp.dot(ds, wd.T, preferred_element_type=jnp.float32).astype(jnp.bfloat16)
        gate_k, up_k, back_k = lax.optimization_barrier((gate_k, up_k, back_k))
        return (carry[0] + gate_k.astype(jnp.float32), carry[1] + up_k.astype(jnp.float32),
                carry[2] + back_k.astype(jnp.float32)), None

    zeros = jnp.zeros((TOKENS, FF), jnp.float32)
    sums, unused = lax.scan(add_block, (zeros, zeros, zeros), jnp.arange(N_COL, dtype=jnp.int32))
    gate, up, grad_hidden = sums
    sig = 1.0 / (1.0 + jnp.exp(-gate))
    hidden = (gate * sig * up).astype(jnp.bfloat16)
    grad_gate_act = (grad_hidden * up * sig * (1.0 + gate * (1.0 - sig))).astype(jnp.bfloat16)
    grad_up_act = (grad_hidden * gate * sig).astype(jnp.bfloat16)
    grad_down = jnp.dot(hidden.T, grad_out, preferred_element_type=jnp.float32).astype(jnp.bfloat16)
    grad_gate = jnp.dot(tokens_in.T, grad_gate_act, preferred_element_type=jnp.float32).astype(jnp.bfloat16)
    grad_up = jnp.dot(tokens_in.T, grad_up_act, preferred_element_type=jnp.float32).astype(jnp.bfloat16)
    grad_input = (jnp.dot(grad_gate_act, w_gate.T, preferred_element_type=jnp.float32)
                  + jnp.dot(grad_up_act, w_up.T, preferred_element_type=jnp.float32)).astype(jnp.bfloat16)
    return grad_input, grad_gate, grad_up, grad_down
```

```python
import functools

import jax
import jax.numpy as jnp
from jax import lax
from jax.experimental import pallas as pl
from jax.experimental.pallas import tpu as pltpu
from jax.sharding import PartitionSpec as P

MESH = pl.DeviceIdType.MESH
CHUNK = 512
EARLY = 4
GROUPS = 4
SLACK = 2
BF16 = jnp.bfloat16
F32 = jnp.float32


def dot_nt(left, right):
    return lax.dot_general(left, right, (((1,), (1,)), ((), ())), preferred_element_type=F32)


def tile(size, most):
    while size % most:
        most //= 2
    return most


def kernel(
    cfg,
    x_in, g_in, wg_hbm, wu_hbm, wd_hbm,
    gi_ref, gg_hbm, gu_hbm, gd_hbm,
    x_ref, xt_ref, g_ref, wf, wdf, wb, part, prec, rs_in, rs_out, act, acc, hid_t, og, od,
    row_send, row_recv, wf_sem, wb_sem, out_sem,
    p_send, p_recv, rs_send, rs_recv, an_send, an_recv, ap_send, ap_recv, tick,
):
    R, Z, NC, C, K, S1, S2, S3 = cfg
    T, DL = x_ref.shape
    N = NC * GROUPS
    G = T // GROUPS
    H, Q = G // 2, G // 4
    RPG = R // GROUPS
    me = lax.axis_index("col")
    pos = lax.div(me, 2)
    core = lax.rem(me, 2)
    partner = me + 1 - 2 * core
    has_left, has_right = pos > 0, pos < Z - 1
    left = jnp.where(has_left, me - 2, partner)
    right = jnp.where(has_right, me + 2, partner)

    def signal(sem, dev):
        pl.semaphore_signal(sem, inc=1, device_id={"col": dev}, device_id_type=MESH)

    row = lax.axis_index("row")
    TR = x_in.shape[0]
    barrier = pltpu.get_barrier_semaphore()
    for k in range(1, R):
        pl.semaphore_signal(
            barrier, inc=1, device_id={"row": lax.rem(row + k, R)}, device_id_type=MESH
        )
    signal(barrier, partner)

    @pl.when(has_left)
    def _():
        signal(barrier, left)

    @pl.when(has_right)
    def _():
        signal(barrier, right)

    pl.semaphore_wait(barrier, R + jnp.where(has_left, 1, 0) + jnp.where(has_right, 1, 0))

    def block(j):
        early = lax.div(jnp.maximum(j - K, 0), GROUPS - 1)
        return jnp.where(j < K, j, jnp.where(j < K * GROUPS, early, lax.div(j, GROUPS)))

    def group(j):
        early = 1 + lax.rem(jnp.maximum(j - K, 0), GROUPS - 1)
        k = jnp.where(j < K, 0, jnp.where(j < K * GROUPS, early, lax.rem(j, GROUPS)))
        mine = lax.div(row, RPG)
        total, bit = 0, 1
        while bit < GROUPS:
            total = total + bit * lax.rem(lax.div(mine, bit) + lax.div(k, bit), 2)
            bit *= 2
        return total

    def load(j):
        return jnp.where(j < K, j, K + block(j))

    def load_block(n):
        return jnp.where(n < K, n, n - K)

    def fresh(j):
        later = lax.rem(jnp.maximum(j - K, 0), GROUPS - 1) == 0
        return jnp.logical_or(
            j < K,
            jnp.where(j < K * GROUPS, later, lax.rem(j, GROUPS) == 0),
        )

    def peer(k):
        total, bit = 0, 1
        while bit < R:
            total = total + bit * lax.rem(lax.div(row, bit) + (k // bit) % 2, 2)
            bit *= 2
        return total

    def remote(src, dst, ssem, rsem, dev):
        return pltpu.make_async_remote_copy(
            src_ref=src, dst_ref=dst, send_sem=ssem, recv_sem=rsem,
            device_id={"col": dev}, device_id_type=MESH,
        )

    def cols(c):
        return pl.ds(pl.multiple_of(c * C, C), C)

    def wf_copies(n):
        s, c = lax.rem(n, 2), load_block(n)
        return (
            pltpu.make_async_copy(wg_hbm.at[:, cols(c)], wf.at[s, :, pl.ds(0, C)], wf_sem.at[s, 0]),
            pltpu.make_async_copy(wu_hbm.at[:, cols(c)], wf.at[s, :, pl.ds(C, C)], wf_sem.at[s, 1]),
            pltpu.make_async_copy(wd_hbm.at[cols(c), :], wdf.at[s], wf_sem.at[s, 2]),
        )

    def wb_copies(n):
        s, c = lax.rem(n, 2), load_block(n)
        return (
            pltpu.make_async_copy(wg_hbm.at[:, cols(c)], wb.at[s, :, pl.ds(0, C)], wb_sem.at[s, 0]),
            pltpu.make_async_copy(wu_hbm.at[:, cols(c)], wb.at[s, :, pl.ds(C, C)], wb_sem.at[s, 1]),
        )

    DH, CH = DL // GROUPS, C // GROUPS

    def out_copies(u):
        c, q, h = lax.div(u, GROUPS), lax.rem(u, GROUPS), lax.rem(u, 2)
        rows = pl.ds(pl.multiple_of(q * DH, DH), DH)
        units = pl.ds(pl.multiple_of(c * C + q * CH, CH), CH)
        return (
            pltpu.make_async_copy(og.at[h, :, pl.ds(0, C)], gg_hbm.at[rows, cols(c)], out_sem.at[h, 0]),
            pltpu.make_async_copy(og.at[h, :, pl.ds(C, C)], gu_hbm.at[rows, cols(c)], out_sem.at[h, 1]),
            pltpu.make_async_copy(od.at[h], gd_hbm.at[units, :], out_sem.at[h, 2]),
        )

    def start(copies):
        for copy in copies:
            copy.start()

    def wait(copies):
        for copy in copies:
            copy.wait()

    def half_rows(which):
        return pl.ds(pl.multiple_of(which * H, H), H)

    def pair_copy(j):
        s1 = lax.rem(j, S1)
        s = lax.rem(j, 2)
        return remote(
            part.at[s1, half_rows(1 - core), :], prec.at[s1], p_send.at[s], p_recv.at[s1], partner
        )

    def sum_copy(side, j):
        s = lax.rem(j, S2)
        dev = left if side == 0 else right
        return remote(rs_out.at[side, s], rs_in.at[side, s], rs_send.at[side, s], rs_recv.at[side, s], dev)

    def act_part(side, j):
        rows = pl.ds(pl.multiple_of(group(j) * G + core * H + side * Q, Q), Q)
        return act.at[lax.rem(block(j), S3), rows, :]

    def act_copy(side, j):
        s = lax.rem(j, S1)
        rows = act_part(side, j)
        dev = right if side == 0 else left
        return remote(rows, rows, an_send.at[side, s], an_recv.at[side, s], dev)

    def act_pair_copy(side, j):
        s = lax.rem(j, S1)
        rows = act_part(side, j)
        return remote(rows, rows, ap_send.at[side, s], ap_recv.at[side, s], partner)

    def act_forwards(side):
        return has_right if side == 0 else has_left

    RB = 16 if Q % 16 == 0 else Q

    def over_rows(side, j, add_in, finish):
        s1, s2, s3 = lax.rem(j, S1), lax.rem(j, S2), lax.rem(block(j), S3)
        first = group(j) * G + core * H + side * Q

        def body(i, carry):
            mine = pl.ds(pl.multiple_of(core * H + side * Q + i * RB, RB), RB)
            local = pl.ds(pl.multiple_of(side * Q + i * RB, RB), RB)
            piece = pl.ds(pl.multiple_of(i * RB, RB), RB)

            def total(n):
                at = pl.ds(n * C, C)
                value = part[s1, mine, at].astype(F32) + prec[s1, local, at].astype(F32)
                if add_in:
                    value = value + rs_in[side, s2, piece, at].astype(F32)
                return value

            if finish:
                gate, up_val, grad_hidden = total(0), total(1), total(2)
                sig = 1.0 / (1.0 + jnp.exp(-gate))
                dst = pl.ds(pl.multiple_of(first + i * RB, RB), RB)
                act[s3, dst, pl.ds(0, C)] = (
                    grad_hidden * up_val * sig * (1.0 + gate * (1.0 - sig))
                ).astype(BF16)
                act[s3, dst, pl.ds(C, C)] = (grad_hidden * gate * sig).astype(BF16)
                act[s3, dst, pl.ds(2 * C, C)] = (gate * sig * up_val).astype(BF16)
            else:
                for n in range(3):
                    rs_out[side, s2, piece, pl.ds(n * C, C)] = total(n).astype(BF16)
            return carry

        lax.fori_loop(0, Q // RB, body, 0)

    def sums(t, side):
        order = pos if side == 1 else Z - 1 - pos
        j = t - 1 - order
        live = jnp.logical_and(j >= 0, j < N)

        @pl.when(jnp.logical_and(live, order > 0))
        def _():
            sum_copy(side, j).wait_recv()

        @pl.when(jnp.logical_and(live, order < Z - 1))
        def _():
            @pl.when(j >= S2)
            def _():
                sum_copy(side, j).wait_send()

            @pl.when(order == 0)
            def _():
                over_rows(side, j, False, False)

            @pl.when(order > 0)
            def _():
                over_rows(side, j, True, False)

            sum_copy(side, j).start()

        @pl.when(jnp.logical_and(live, order == Z - 1))
        def _():
            over_rows(side, j, Z > 1, True)

            @pl.when(act_forwards(side))
            def _():
                act_copy(side, j).start()

            act_pair_copy(side, j).start()

    def spread(t, side):
        order = pos if side == 0 else Z - 1 - pos
        j = t - Z - order

        @pl.when(jnp.logical_and(order > 0, jnp.logical_and(j >= 0, j < N)))
        def _():
            act_copy(side, j).wait_recv()

            @pl.when(act_forwards(side))
            def _():
                act_copy(side, j).start()

            act_pair_copy(side, j).start()

    NB = tile(C, 256)
    GB = tile(DH, 256)
    AB = tile(DL, 256)

    def forward(j):
        n, s1 = load(j), lax.rem(j, S1)
        s = lax.rem(n, 2)

        @pl.when(jnp.logical_and(j + 1 < N, fresh(j + 1)))
        def _():
            start(wf_copies(load(j + 1)))

        @pl.when(fresh(j))
        def _():
            wait(wf_copies(n))

        for k in range(1, GROUPS):
            @pl.when(j == K + k - 1)
            def _():
                for m in range(k * RPG, (k + 1) * RPG):
                    row_copy(0, m, peer(m)).wait_recv()
                    row_copy(1, m, peer(m)).wait_recv()

        @pl.when(j >= 2)
        def _():
            pair_copy(j).wait_send()

        src = pl.ds(pl.multiple_of(group(j) * G, G), G)

        def up(i, carry):
            at = pl.ds(pl.multiple_of(i * NB, NB), NB)
            part[s1, :, at] = jnp.dot(
                x_ref[src, :], wf[s, :, at], preferred_element_type=F32
            ).astype(BF16)
            return carry

        lax.fori_loop(0, 2 * C // NB, up, 0)

        def back(i, carry):
            rows = pl.ds(pl.multiple_of(i * NB, NB), NB)
            at = pl.ds(pl.multiple_of(2 * C + i * NB, NB), NB)
            part[s1, :, at] = dot_nt(g_ref[src, :], wdf[s, rows, :]).astype(BF16)
            return carry

        lax.fori_loop(0, C // NB, back, 0)
        pair_copy(j).start()

    def inputs(j):
        s, s3 = lax.rem(load(j), 2), lax.rem(block(j), S3)
        for side in range(2):
            act_pair_copy(side, j).wait_recv()

        @pl.when(fresh(j))
        def _():
            wait(wb_copies(load(j)))

        rows = pl.ds(pl.multiple_of(group(j) * G, G), G)

        def add(i, carry):
            at = pl.ds(pl.multiple_of(i * AB, AB), AB)
            acc[rows, at] += dot_nt(act[s3, rows, pl.ds(0, 2 * C)], wb[s, at, :])
            return carry

        lax.fori_loop(0, DL // AB, add, 0)
        for side in range(2):
            @pl.when(act_forwards(side))
            def _():
                act_copy(side, j).wait_send()

            act_pair_copy(side, j).wait_send()

    def grads(u):
        c, q, h = lax.div(u, GROUPS), lax.rem(u, GROUPS), lax.rem(u, 2)
        s3 = lax.rem(c, S3)

        @pl.when(u >= 2)
        def _():
            wait(out_copies(u))

        @pl.when(c == 0)
        def _():
            def turn(i, carry):
                rows = pl.ds(pl.multiple_of(q * DH + i * GB, GB), GB)
                xt_ref[rows, :] = x_ref[:, rows].T
                return carry

            lax.fori_loop(0, DH // GB, turn, 0)

        hid_t[...] = act[s3, :, pl.ds(pl.multiple_of(2 * C + q * CH, CH), CH)].T

        def weights(i, carry):
            rows = pl.ds(pl.multiple_of(i * GB, GB), GB)
            src = pl.ds(pl.multiple_of(q * DH + i * GB, GB), GB)

            def across(n, carry):
                at = pl.ds(pl.multiple_of(n * NB, NB), NB)
                og[h, rows, at] = jnp.dot(
                    xt_ref[src, :], act[s3, :, at], preferred_element_type=F32
                ).astype(BF16)
                return carry

            return lax.fori_loop(0, 2 * C // NB, across, carry)

        lax.fori_loop(0, DH // GB, weights, 0)

        def down(i, carry):
            at = pl.ds(pl.multiple_of(i * AB, AB), AB)
            od[h, :, at] = jnp.dot(
                hid_t[...], g_ref[:, at], preferred_element_type=F32
            ).astype(BF16)
            return carry

        lax.fori_loop(0, DL // AB, down, 0)
        start(out_copies(u))

    def tick_wait():
        @pl.when(has_left)
        def _():
            pl.semaphore_wait(tick.at[0], 1)

        @pl.when(has_right)
        def _():
            pl.semaphore_wait(tick.at[1], 1)

        pl.semaphore_wait(tick.at[2], 1)

    def row_copy(which, k, owner):
        src, dst = ((x_in, x_ref), (g_in, g_ref))[which]
        rows = pl.ds(pl.multiple_of(owner * TR, TR), TR)
        return pltpu.make_async_remote_copy(
            src_ref=src, dst_ref=dst.at[rows, :],
            send_sem=row_send.at[which, k], recv_sem=row_recv.at[which, k],
            device_id={"row": peer(k)}, device_id_type=MESH,
        )

    for k in range(1, R):
        for which in range(2):
            row_copy(which, k, row).start()
    start(wf_copies(0))
    mine = pl.ds(pl.multiple_of(row * TR, TR), TR)
    x_ref[mine, :] = x_in[...]
    g_ref[mine, :] = g_in[...]
    acc[...] = jnp.zeros_like(acc)
    steps = N + 2 * Z + 1
    for k in range(1, RPG):
        for which in range(2):
            row_copy(which, k, peer(k)).wait_recv()

    def step(t, carry):
        @pl.when(t >= SLACK)
        def _():
            tick_wait()

        nxt = t + 1 - 2 * Z

        @pl.when(jnp.logical_and(jnp.logical_and(nxt >= 0, nxt < N), fresh(nxt)))
        def _():
            start(wb_copies(load(nxt)))

        @pl.when(jnp.logical_and(t >= 1, t - 1 < N))
        def _():
            pair_copy(t - 1).wait_recv()

        sums(t, 0)
        sums(t, 1)

        @pl.when(t < N)
        def _():
            forward(t)

        spread(t, 0)
        spread(t, 1)
        b = t - 2 * Z

        @pl.when(jnp.logical_and(b >= 0, b < N))
        def _():
            inputs(b)

        late = jnp.maximum(b - (N - GROUPS), 0)
        u = jnp.minimum(b, N - GROUPS) - (K + 2) + 2 * late
        more = jnp.where(b >= N - GROUPS, 2, 1)

        def quarter(i, carry):
            grads(u + i)
            return carry

        @pl.when(u >= 0)
        def _():
            lax.fori_loop(0, more, quarter, 0)

        signal(tick.at[2], partner)

        @pl.when(has_left)
        def _():
            signal(tick.at[1], left)

        @pl.when(has_right)
        def _():
            signal(tick.at[0], right)

        return carry

    lax.fori_loop(0, steps, step, 0)
    for _ in range(SLACK):
        tick_wait()
    for which in range(2):
        for k in range(1, R):
            row_copy(which, k, row).wait_send()
    for j in range(max(N - 2, 0), N):
        pair_copy(j).wait_send()
    for u in range(N - 2, N):
        wait(out_copies(u))
    for side in range(2):
        @pl.when(has_left if side == 0 else has_right)
        def _():
            for j in range(max(N - S2, 0), N):
                sum_copy(side, j).wait_send()

    gi_ref[...] = acc[...].astype(BF16)


def fused(n_row, n_col, x, g, wg, wu, wd):
    T, DL = x.shape[0] * n_row, x.shape[1]
    F = wg.shape[1]
    C = tile(F, CHUNK)
    Z, NC = n_col // 2, F // C
    K = EARLY
    S1, S2 = Z + SLACK, SLACK + 1
    S3 = max(K, -(-(Z + K + GROUPS + 1 + SLACK) // GROUPS))
    G = T // GROUPS
    H, Q = G // 2, G // 4
    vm = pl.BlockSpec(memory_space=pltpu.VMEM)
    hbm = pl.BlockSpec(memory_space=pl.ANY)
    dma = pltpu.SemaphoreType.DMA
    return pl.pallas_call(
        functools.partial(kernel, (n_row, Z, NC, C, K, S1, S2, S3)),
        out_shape=(
            jax.ShapeDtypeStruct((T, DL), BF16),
            jax.ShapeDtypeStruct((DL, F), BF16),
            jax.ShapeDtypeStruct((DL, F), BF16),
            jax.ShapeDtypeStruct((F, DL), BF16),
        ),
        in_specs=[vm, vm, hbm, hbm, hbm],
        out_specs=(vm, hbm, hbm, hbm),
        scratch_shapes=[
            pltpu.VMEM((T, DL), BF16),
            pltpu.VMEM((DL, T), BF16),
            pltpu.VMEM((T, DL), BF16),
            pltpu.VMEM((2, DL, 2 * C), BF16),
            pltpu.VMEM((2, C, DL), BF16),
            pltpu.VMEM((2, DL, 2 * C), BF16),
            pltpu.VMEM((S1, G, 3 * C), BF16),
            pltpu.VMEM((S1, H, 3 * C), BF16),
            pltpu.VMEM((2, S2, Q, 3 * C), BF16),
            pltpu.VMEM((2, S2, Q, 3 * C), BF16),
            pltpu.VMEM((S3, T, 3 * C), BF16),
            pltpu.VMEM((T, DL), F32),
            pltpu.VMEM((C // GROUPS, T), BF16),
            pltpu.VMEM((2, DL // GROUPS, 2 * C), BF16),
            pltpu.VMEM((2, C // GROUPS, DL), BF16),
            dma((2, n_row)), dma((2, n_row)),
            dma((2, 3)), dma((2, 2)), dma((2, 3)),
            dma((2,)), dma((S1,)),
            dma((2, S2)), dma((2, S2)),
            dma((2, S1)), dma((2, S1)),
            dma((2, S1)), dma((2, S1)),
            pltpu.SemaphoreType.REGULAR((3,)),
        ],
        compiler_params=pltpu.CompilerParams(
            collective_id=0, has_side_effects=True, vmem_limit_bytes=60 * 1024 * 1024
        ),
    )(x, g, wg, wu, wd)


def move(a_in, b_in, c_in, a_out, b_out, c_out):
    a_out[...] = a_in[...]
    b_out[...] = b_in[...]
    c_out[...] = c_in[...]


def settle(arrays):
    parts = 8
    specs = [pl.BlockSpec((a.shape[0] // parts, a.shape[1]), lambda i: (i, 0)) for a in arrays]
    size = sum(a.size * a.dtype.itemsize for a in arrays)
    return pl.pallas_call(
        move,
        grid=(parts,),
        out_shape=tuple(jax.ShapeDtypeStruct(a.shape, a.dtype) for a in arrays),
        in_specs=specs,
        out_specs=tuple(specs),
        cost_estimate=pl.CostEstimate(flops=0, bytes_accessed=2 * size, transcendentals=0),
        compiler_params=pltpu.CompilerParams(vmem_limit_bytes=60 * 1024 * 1024),
    )(*arrays)


def solution(mesh):
    n_row, n_col = mesh.shape["row"], mesh.shape["col"]

    def local(tokens_in, grad_out, w_gate, w_up, w_down):
        acc, *grads = fused(n_row, n_col, tokens_in, grad_out, w_gate, w_up, w_down)
        grad_input = lax.psum_scatter(acc, "row", scatter_dimension=0, tiled=True)
        return (grad_input, *settle(grads))

    return jax.shard_map(
        local,
        mesh=mesh,
        in_specs=(
            P("row", "col"),
            P("row", "col"),
            P("col", "row"),
            P("col", "row"),
            P("row", "col"),
        ),
        out_specs=(P("row", "col"), P("col", "row"), P("col", "row"), P("row", "col")),
        check_vma=False,
    )
```

```python
import functools

import jax
import jax.numpy as jnp
from jax import lax
from jax.experimental import pallas as pl
from jax.experimental.pallas import tpu as pltpu
from jax.sharding import PartitionSpec as P

MESH = pl.DeviceIdType.MESH
CHUNK = 512
EARLY = 4
GROUPS = 4
SLACK = 2
BF16 = jnp.bfloat16
F32 = jnp.float32


def dot_nt(left, right):
    return lax.dot_general(left, right, (((1,), (1,)), ((), ())), preferred_element_type=F32)


def tile(size, most):
    while size % most:
        most //= 2
    return most


def kernel(
    cfg,
    x_in, g_in, wg_hbm, wu_hbm, wd_hbm,
    gi_ref, gg_hbm, gu_hbm, gd_hbm,
    x_ref, xt_ref, g_ref, wf, wdf, wb, part, prec, rs_in, rs_out, act, acc, hid_t, og, od,
    row_send, row_recv, wf_sem, wb_sem, out_sem,
    p_send, p_recv, rs_send, rs_recv, an_send, an_recv, ap_send, ap_recv, tick,
):
    R, Z, NC, C, K, S1, S2, S3 = cfg
    T, DL = x_ref.shape
    N = NC * GROUPS
    G = T // GROUPS
    H, Q = G // 2, G // 4
    RPG = R // GROUPS
    me = lax.axis_index("col")
    pos = lax.div(me, 2)
    core = lax.rem(me, 2)
    partner = me + 1 - 2 * core
    has_left, has_right = pos > 0, pos < Z - 1
    left = jnp.where(has_left, me - 2, partner)
    right = jnp.where(has_right, me + 2, partner)

    def signal(sem, dev):
        pl.semaphore_signal(sem, inc=1, device_id={"col": dev}, device_id_type=MESH)

    row = lax.axis_index("row")
    TR = x_in.shape[0]
    barrier = pltpu.get_barrier_semaphore()
    for k in range(1, R):
        pl.semaphore_signal(
            barrier, inc=1, device_id={"row": lax.rem(row + k, R)}, device_id_type=MESH
        )
    signal(barrier, partner)

    @pl.when(has_left)
    def _():
        signal(barrier, left)

    @pl.when(has_right)
    def _():
        signal(barrier, right)

    pl.semaphore_wait(barrier, R + jnp.where(has_left, 1, 0) + jnp.where(has_right, 1, 0))

    def block(j):
        early = lax.div(jnp.maximum(j - K, 0), GROUPS - 1)
        return jnp.where(j < K, j, jnp.where(j < K * GROUPS, early, lax.div(j, GROUPS)))

    def group(j):
        early = 1 + lax.rem(jnp.maximum(j - K, 0), GROUPS - 1)
        k = jnp.where(j < K, 0, jnp.where(j < K * GROUPS, early, lax.rem(j, GROUPS)))
        mine = lax.div(row, RPG)
        total, bit = 0, 1
        while bit < GROUPS:
            total = total + bit * lax.rem(lax.div(mine, bit) + lax.div(k, bit), 2)
            bit *= 2
        return total

    def load(j):
        return jnp.where(j < K, j, K + block(j))

    def load_block(n):
        return jnp.where(n < K, n, n - K)

    def fresh(j):
        later = lax.rem(jnp.maximum(j - K, 0), GROUPS - 1) == 0
        return jnp.logical_or(
            j < K,
            jnp.where(j < K * GROUPS, later, lax.rem(j, GROUPS) == 0),
        )

    def peer(k):
        total, bit = 0, 1
        while bit < R:
            total = total + bit * lax.rem(lax.div(row, bit) + (k // bit) % 2, 2)
            bit *= 2
        return total

    def remote(src, dst, ssem, rsem, dev):
        return pltpu.make_async_remote_copy(
            src_ref=src, dst_ref=dst, send_sem=ssem, recv_sem=rsem,
            device_id={"col": dev}, device_id_type=MESH,
        )

    def cols(c):
        return pl.ds(pl.multiple_of(c * C, C), C)

    def wf_copies(n):
        s, c = lax.rem(n, 2), load_block(n)
        return (
            pltpu.make_async_copy(wg_hbm.at[:, cols(c)], wf.at[s, :, pl.ds(0, C)], wf_sem.at[s, 0]),
            pltpu.make_async_copy(wu_hbm.at[:, cols(c)], wf.at[s, :, pl.ds(C, C)], wf_sem.at[s, 1]),
            pltpu.make_async_copy(wd_hbm.at[cols(c), :], wdf.at[s], wf_sem.at[s, 2]),
        )

    def wb_copies(n):
        s, c = lax.rem(n, 2), load_block(n)
        return (
            pltpu.make_async_copy(wg_hbm.at[:, cols(c)], wb.at[s, :, pl.ds(0, C)], wb_sem.at[s, 0]),
            pltpu.make_async_copy(wu_hbm.at[:, cols(c)], wb.at[s, :, pl.ds(C, C)], wb_sem.at[s, 1]),
        )

    DH, CH = DL // GROUPS, C // GROUPS

    def out_copies(u):
        c, q, h = lax.div(u, GROUPS), lax.rem(u, GROUPS), lax.rem(u, 2)
        rows = pl.ds(pl.multiple_of(q * DH, DH), DH)
        units = pl.ds(pl.multiple_of(c * C + q * CH, CH), CH)
        return (
            pltpu.make_async_copy(og.at[h, :, pl.ds(0, C)], gg_hbm.at[rows, cols(c)], out_sem.at[h, 0]),
            pltpu.make_async_copy(og.at[h, :, pl.ds(C, C)], gu_hbm.at[rows, cols(c)], out_sem.at[h, 1]),
            pltpu.make_async_copy(od.at[h], gd_hbm.at[units, :], out_sem.at[h, 2]),
        )

    def start(copies):
        for copy in copies:
            copy.start()

    def wait(copies):
        for copy in copies:
            copy.wait()

    def half_rows(which):
        return pl.ds(pl.multiple_of(which * H, H), H)

    def pair_copy(j):
        s1 = lax.rem(j, S1)
        s = lax.rem(j, 2)
        return remote(
            part.at[s1, half_rows(1 - core), :], prec.at[s1], p_send.at[s], p_recv.at[s1], partner
        )

    def sum_copy(side, j):
        s = lax.rem(j, S2)
        dev = left if side == 0 else right
        return remote(rs_out.at[side, s], rs_in.at[side, s], rs_send.at[side, s], rs_recv.at[side, s], dev)

    def act_part(side, j):
        rows = pl.ds(pl.multiple_of(group(j) * G + core * H + side * Q, Q), Q)
        return act.at[lax.rem(block(j), S3), rows, :]

    def act_copy(side, j):
        s = lax.rem(j, S1)
        rows = act_part(side, j)
        dev = right if side == 0 else left
        return remote(rows, rows, an_send.at[side, s], an_recv.at[side, s], dev)

    def act_pair_copy(side, j):
        s = lax.rem(j, S1)
        rows = act_part(side, j)
        return remote(rows, rows, ap_send.at[side, s], ap_recv.at[side, s], partner)

    def act_forwards(side):
        return has_right if side == 0 else has_left

    RB = 16 if Q % 16 == 0 else Q

    def over_rows(side, j, add_in, finish):
        s1, s2, s3 = lax.rem(j, S1), lax.rem(j, S2), lax.rem(block(j), S3)
        first = group(j) * G + core * H + side * Q

        def body(i, carry):
            mine = pl.ds(pl.multiple_of(core * H + side * Q + i * RB, RB), RB)
            local = pl.ds(pl.multiple_of(side * Q + i * RB, RB), RB)
            piece = pl.ds(pl.multiple_of(i * RB, RB), RB)

            def total(n):
                at = pl.ds(n * C, C)
                value = part[s1, mine, at].astype(F32) + prec[s1, local, at].astype(F32)
                if add_in:
                    value = value + rs_in[side, s2, piece, at].astype(F32)
                return value

            if finish:
                gate, up_val, grad_hidden = total(0), total(1), total(2)
                sig = 1.0 / (1.0 + jnp.exp(-gate))
                dst = pl.ds(pl.multiple_of(first + i * RB, RB), RB)
                act[s3, dst, pl.ds(0, C)] = (
                    grad_hidden * up_val * sig * (1.0 + gate * (1.0 - sig))
                ).astype(BF16)
                act[s3, dst, pl.ds(C, C)] = (grad_hidden * gate * sig).astype(BF16)
                act[s3, dst, pl.ds(2 * C, C)] = (gate * sig * up_val).astype(BF16)
            else:
                for n in range(3):
                    rs_out[side, s2, piece, pl.ds(n * C, C)] = total(n).astype(BF16)
            return carry

        lax.fori_loop(0, Q // RB, body, 0)

    def sums(t, side):
        order = pos if side == 1 else Z - 1 - pos
        j = t - 1 - order
        live = jnp.logical_and(j >= 0, j < N)

        @pl.when(jnp.logical_and(live, order > 0))
        def _():
            sum_copy(side, j).wait_recv()

        @pl.when(jnp.logical_and(live, order < Z - 1))
        def _():
            @pl.when(j >= S2)
            def _():
                sum_copy(side, j).wait_send()

            @pl.when(order == 0)
            def _():
                over_rows(side, j, False, False)

            @pl.when(order > 0)
            def _():
                over_rows(side, j, True, False)

            sum_copy(side, j).start()

        @pl.when(jnp.logical_and(live, order == Z - 1))
        def _():
            over_rows(side, j, Z > 1, True)

            @pl.when(act_forwards(side))
            def _():
                act_copy(side, j).start()

            act_pair_copy(side, j).start()

    def spread(t, side):
        order = pos if side == 0 else Z - 1 - pos
        j = t - Z - order

        @pl.when(jnp.logical_and(order > 0, jnp.logical_and(j >= 0, j < N)))
        def _():
            act_copy(side, j).wait_recv()

            @pl.when(act_forwards(side))
            def _():
                act_copy(side, j).start()

            act_pair_copy(side, j).start()

    NB = tile(C, 256)
    GB = tile(DH, 256)
    AB = tile(DL, 256)

    def forward(j):
        n, s1 = load(j), lax.rem(j, S1)
        s = lax.rem(n, 2)

        @pl.when(jnp.logical_and(j + 1 < N, fresh(j + 1)))
        def _():
            start(wf_copies(load(j + 1)))

        @pl.when(fresh(j))
        def _():
            wait(wf_copies(n))

        for k in range(1, GROUPS):
            @pl.when(j == K + k - 1)
            def _():
                for m in range(k * RPG, (k + 1) * RPG):
                    row_copy(0, m, peer(m)).wait_recv()
                    row_copy(1, m, peer(m)).wait_recv()

        @pl.when(j >= 2)
        def _():
            pair_copy(j).wait_send()

        src = pl.ds(pl.multiple_of(group(j) * G, G), G)

        def up(i, carry):
            at = pl.ds(pl.multiple_of(i * NB, NB), NB)
            part[s1, :, at] = jnp.dot(
                x_ref[src, :], wf[s, :, at], preferred_element_type=F32
            ).astype(BF16)
            return carry

        lax.fori_loop(0, 2 * C // NB, up, 0, unroll=True)

        def back(i, carry):
            rows = pl.ds(pl.multiple_of(i * NB, NB), NB)
            at = pl.ds(pl.multiple_of(2 * C + i * NB, NB), NB)
            part[s1, :, at] = dot_nt(g_ref[src, :], wdf[s, rows, :]).astype(BF16)
            return carry

        lax.fori_loop(0, C // NB, back, 0, unroll=True)
        pair_copy(j).start()

    def inputs(j):
        s, s3 = lax.rem(load(j), 2), lax.rem(block(j), S3)
        for side in range(2):
            act_pair_copy(side, j).wait_recv()

        @pl.when(fresh(j))
        def _():
            wait(wb_copies(load(j)))

        rows = pl.ds(pl.multiple_of(group(j) * G, G), G)

        def add(i, carry):
            at = pl.ds(pl.multiple_of(i * AB, AB), AB)
            acc[rows, at] += dot_nt(act[s3, rows, pl.ds(0, 2 * C)], wb[s, at, :])
            return carry

        lax.fori_loop(0, DL // AB, add, 0, unroll=True)
        for side in range(2):
            @pl.when(act_forwards(side))
            def _():
                act_copy(side, j).wait_send()

            act_pair_copy(side, j).wait_send()

    def grads(u):
        c, q, h = lax.div(u, GROUPS), lax.rem(u, GROUPS), lax.rem(u, 2)
        s3 = lax.rem(c, S3)

        @pl.when(u >= 2)
        def _():
            wait(out_copies(u))

        @pl.when(c == 0)
        def _():
            def turn(i, carry):
                rows = pl.ds(pl.multiple_of(q * DH + i * GB, GB), GB)
                xt_ref[rows, :] = x_ref[:, rows].T
                return carry

            lax.fori_loop(0, DH // GB, turn, 0)

        hid_t[...] = act[s3, :, pl.ds(pl.multiple_of(2 * C + q * CH, CH), CH)].T

        def weights(i, carry):
            rows = pl.ds(pl.multiple_of(i * GB, GB), GB)
            src = pl.ds(pl.multiple_of(q * DH + i * GB, GB), GB)

            def across(n, carry):
                at = pl.ds(pl.multiple_of(n * NB, NB), NB)
                og[h, rows, at] = jnp.dot(
                    xt_ref[src, :], act[s3, :, at], preferred_element_type=F32
                ).astype(BF16)
                return carry

            return lax.fori_loop(0, 2 * C // NB, across, carry, unroll=True)

        lax.fori_loop(0, DH // GB, weights, 0)

        def down(i, carry):
            at = pl.ds(pl.multiple_of(i * AB, AB), AB)
            od[h, :, at] = jnp.dot(
                hid_t[...], g_ref[:, at], preferred_element_type=F32
            ).astype(BF16)
            return carry

        lax.fori_loop(0, DL // AB, down, 0, unroll=True)
        start(out_copies(u))

    def tick_wait():
        @pl.when(has_left)
        def _():
            pl.semaphore_wait(tick.at[0], 1)

        @pl.when(has_right)
        def _():
            pl.semaphore_wait(tick.at[1], 1)

        pl.semaphore_wait(tick.at[2], 1)

    def row_copy(which, k, owner):
        src, dst = ((x_in, x_ref), (g_in, g_ref))[which]
        rows = pl.ds(pl.multiple_of(owner * TR, TR), TR)
        return pltpu.make_async_remote_copy(
            src_ref=src, dst_ref=dst.at[rows, :],
            send_sem=row_send.at[which, k], recv_sem=row_recv.at[which, k],
            device_id={"row": peer(k)}, device_id_type=MESH,
        )

    for k in range(1, R):
        for which in range(2):
            row_copy(which, k, row).start()
    start(wf_copies(0))
    mine = pl.ds(pl.multiple_of(row * TR, TR), TR)
    x_ref[mine, :] = x_in[...]
    g_ref[mine, :] = g_in[...]
    acc[...] = jnp.zeros_like(acc)
    steps = N + 2 * Z + 1
    for k in range(1, RPG):
        for which in range(2):
            row_copy(which, k, peer(k)).wait_recv()

    def step(t, carry):
        @pl.when(t >= SLACK)
        def _():
            tick_wait()

        nxt = t + 1 - 2 * Z

        @pl.when(jnp.logical_and(jnp.logical_and(nxt >= 0, nxt < N), fresh(nxt)))
        def _():
            start(wb_copies(load(nxt)))

        @pl.when(jnp.logical_and(t >= 1, t - 1 < N))
        def _():
            pair_copy(t - 1).wait_recv()

        sums(t, 0)
        sums(t, 1)

        @pl.when(t < N)
        def _():
            forward(t)

        spread(t, 0)
        spread(t, 1)
        b = t - 2 * Z

        @pl.when(jnp.logical_and(b >= 0, b < N))
        def _():
            inputs(b)

        late = jnp.maximum(b - (N - GROUPS), 0)
        u = jnp.minimum(b, N - GROUPS) - (K + 2) + 2 * late
        more = jnp.where(b >= N - GROUPS, 2, 1)

        def quarter(i, carry):
            grads(u + i)
            return carry

        @pl.when(u >= 0)
        def _():
            lax.fori_loop(0, more, quarter, 0)

        signal(tick.at[2], partner)

        @pl.when(has_left)
        def _():
            signal(tick.at[1], left)

        @pl.when(has_right)
        def _():
            signal(tick.at[0], right)

        return carry

    lax.fori_loop(0, steps, step, 0)
    for _ in range(SLACK):
        tick_wait()
    for which in range(2):
        for k in range(1, R):
            row_copy(which, k, row).wait_send()
    for j in range(max(N - 2, 0), N):
        pair_copy(j).wait_send()
    for u in range(N - 2, N):
        wait(out_copies(u))
    for side in range(2):
        @pl.when(has_left if side == 0 else has_right)
        def _():
            for j in range(max(N - S2, 0), N):
                sum_copy(side, j).wait_send()

    gi_ref[...] = acc[...].astype(BF16)


def fused(n_row, n_col, x, g, wg, wu, wd):
    T, DL = x.shape[0] * n_row, x.shape[1]
    F = wg.shape[1]
    C = tile(F, CHUNK)
    Z, NC = n_col // 2, F // C
    K = EARLY
    S1, S2 = Z + SLACK, SLACK + 1
    S3 = max(K, -(-(Z + K + GROUPS + 1 + SLACK) // GROUPS))
    G = T // GROUPS
    H, Q = G // 2, G // 4
    vm = pl.BlockSpec(memory_space=pltpu.VMEM)
    hbm = pl.BlockSpec(memory_space=pl.ANY)
    dma = pltpu.SemaphoreType.DMA
    return pl.pallas_call(
        functools.partial(kernel, (n_row, Z, NC, C, K, S1, S2, S3)),
        out_shape=(
            jax.ShapeDtypeStruct((T, DL), BF16),
            jax.ShapeDtypeStruct((DL, F), BF16),
            jax.ShapeDtypeStruct((DL, F), BF16),
            jax.ShapeDtypeStruct((F, DL), BF16),
        ),
        in_specs=[vm, vm, hbm, hbm, hbm],
        out_specs=(vm, hbm, hbm, hbm),
        scratch_shapes=[
            pltpu.VMEM((T, DL), BF16),
            pltpu.VMEM((DL, T), BF16),
            pltpu.VMEM((T, DL), BF16),
            pltpu.VMEM((2, DL, 2 * C), BF16),
            pltpu.VMEM((2, C, DL), BF16),
            pltpu.VMEM((2, DL, 2 * C), BF16),
            pltpu.VMEM((S1, G, 3 * C), BF16),
            pltpu.VMEM((S1, H, 3 * C), BF16),
            pltpu.VMEM((2, S2, Q, 3 * C), BF16),
            pltpu.VMEM((2, S2, Q, 3 * C), BF16),
            pltpu.VMEM((S3, T, 3 * C), BF16),
            pltpu.VMEM((T, DL), F32),
            pltpu.VMEM((C // GROUPS, T), BF16),
            pltpu.VMEM((2, DL // GROUPS, 2 * C), BF16),
            pltpu.VMEM((2, C // GROUPS, DL), BF16),
            dma((2, n_row)), dma((2, n_row)),
            dma((2, 3)), dma((2, 2)), dma((2, 3)),
            dma((2,)), dma((S1,)),
            dma((2, S2)), dma((2, S2)),
            dma((2, S1)), dma((2, S1)),
            dma((2, S1)), dma((2, S1)),
            pltpu.SemaphoreType.REGULAR((3,)),
        ],
        compiler_params=pltpu.CompilerParams(
            collective_id=0, has_side_effects=True, vmem_limit_bytes=60 * 1024 * 1024
        ),
    )(x, g, wg, wu, wd)


def move(a_in, b_in, c_in, a_out, b_out, c_out):
    a_out[...] = a_in[...]
    b_out[...] = b_in[...]
    c_out[...] = c_in[...]


def settle(arrays):
    parts = 8
    specs = [pl.BlockSpec((a.shape[0] // parts, a.shape[1]), lambda i: (i, 0)) for a in arrays]
    size = sum(a.size * a.dtype.itemsize for a in arrays)
    return pl.pallas_call(
        move,
        grid=(parts,),
        out_shape=tuple(jax.ShapeDtypeStruct(a.shape, a.dtype) for a in arrays),
        in_specs=specs,
        out_specs=tuple(specs),
        cost_estimate=pl.CostEstimate(flops=0, bytes_accessed=2 * size, transcendentals=0),
        compiler_params=pltpu.CompilerParams(vmem_limit_bytes=60 * 1024 * 1024),
    )(*arrays)


def solution(mesh):
    n_row, n_col = mesh.shape["row"], mesh.shape["col"]

    def local(tokens_in, grad_out, w_gate, w_up, w_down):
        acc, *grads = fused(n_row, n_col, tokens_in, grad_out, w_gate, w_up, w_down)
        grad_input = lax.psum_scatter(acc, "row", scatter_dimension=0, tiled=True)
        return (grad_input, *settle(grads))

    return jax.shard_map(
        local,
        mesh=mesh,
        in_specs=(
            P("row", "col"),
            P("row", "col"),
            P("col", "row"),
            P("col", "row"),
            P("row", "col"),
        ),
        out_specs=(P("row", "col"), P("col", "row"), P("col", "row"), P("row", "col")),
        check_vma=False,
    )
```
